256 devices in a mesh: tp: 4 (over z_lo), sy: 8 (over x, core), sx: 8 (over y, z_hi).
Axes of the slice: x: 4, y: 4, z: 8 (z_hi: 2, z_lo: 4; z = z_hi * 4 + z_lo), core: 2. Of those that a mesh axis runs over, the one named last changes fastest.
Arguments:
- queries: bfloat16 [24, 4, 64, 64, 128], P('tp', None, 'sy', 'sx'), may hold values from -8 to 8
- key_vectors: bfloat16 [24, 4, 64, 64, 128], P('tp', None, 'sy', 'sx'), may hold values from -8 to 8
- value_vectors: bfloat16 [24, 4, 64, 64, 128], P('tp', None, 'sy', 'sx'), may hold values from -6 to 6
- out_grad: bfloat16 [24, 4, 64, 64, 128], P('tp', None, 'sy', 'sx'), may hold values from -6 to 6
- cell_valid: int32 [64, 64], replicated, may hold values from 0 to 1, as said below
Outputs:
- query_grad: bfloat16 [24, 4, 64, 64, 128], P('tp', None, 'sy', 'sx')
- key_grad: bfloat16 [24, 4, 64, 64, 128], P('tp', None, 'sy', 'sx')
- value_grad: bfloat16 [24, 4, 64, 64, 128], P('tp', None, 'sy', 'sx')
The draws below stay inside these ranges and needn't reach their ends.
Inputs may be any that keep to these rules, and one draw needn't show every extreme that they name: cell_valid is 1 exactly on one rectangle of cells and 0 elsewhere; the rectangle holds the rows 16 to 59 and the columns 16 to 59.
All inputs are finite; a program needn't handle non-finite values.
Results may differ from the reference program's by a relative error of at most 0.0085.
Values may be sent and summed in bfloat16 or wider, within the bound.
A program may use at most 64 MiB of HBM per device.

```python
import math
import jax
import jax.numpy as jnp
from jax import lax

HEAD_COUNT = 24
HEAD_DIM = 128
FRAMES = 4
TILE_CELLS = 8
GRID_ROWS = 64
GRID_COLUMNS = 64


def draw_queries(key, part):
    sample = jax.random.normal(jax.random.fold_in(key, 1), (HEAD_COUNT, FRAMES, GRID_ROWS, GRID_COLUMNS, HEAD_DIM), jnp.float32)
    sample = jnp.clip(sample, -5.0, 5.0)
    return sample.astype(jnp.bfloat16)


def draw_key_vectors(key, part):
    sample = jax.random.normal(jax.random.fold_in(key, 2), (HEAD_COUNT, FRAMES, GRID_ROWS, GRID_COLUMNS, HEAD_DIM), jnp.float32)
    sample = jnp.clip(sample, -5.0, 5.0)
    return sample.astype(jnp.bfloat16)


def draw_cell_valid(key, part):
    subkeys = jax.random.split(jax.random.fold_in(key, 5), 4)
    upper_edge = jax.random.randint(subkeys[0], (), 0, GRID_ROWS // 4 + 1)
    lower_edge = GRID_ROWS - jax.random.randint(subkeys[1], (), 0, TILE_CELLS // 2 + 1)
    left_edge = jax.random.randint(subkeys[2], (), 0, GRID_COLUMNS // 4 + 1)
    right_edge = GRID_COLUMNS - jax.random.randint(subkeys[3], (), 0, TILE_CELLS // 2 + 1)
    row_number = jnp.arange(GRID_ROWS)
    column_number = jnp.arange(GRID_COLUMNS)
    row_inside = (row_number >= upper_edge) & (row_number < lower_edge)
    column_inside = (column_number >= left_edge) & (column_number < right_edge)
    return (row_inside[:, None] & column_inside[None, :]).astype(jnp.int32)


def steps_of(rng, dims, cuts, smallest, largest):
    loudness, own = 1.0, jax.random.fold_in(rng, 6)
    for dim, parts in cuts:
        draws = jnp.exp(jax.random.uniform(jax.random.fold_in(own, dim), (parts,), jnp.float32, smallest / len(cuts), largest / len(cuts)))
        loudness = loudness * jnp.repeat(draws, dims[dim] // parts).reshape([-1 if axis == dim else 1 for axis in range(len(dims))])
    return loudness


def normal_values(rng, dims, scale, limit, cuts=(), kind=jnp.bfloat16):
    values = scale * jax.random.normal(rng, dims, jnp.float32)
    if cuts:
        values = values * steps_of(rng, dims, cuts, -0.22, 0.18)
    return jnp.clip(values, -limit, limit).astype(kind)


def setup_inputs(seed: int = 0) -> dict:
    splits = jax.random.split(jax.random.key(seed), 6)
    queries = draw_queries(jax.random.fold_in(splits[5], 71), 0)
    key_vectors = draw_key_vectors(jax.random.fold_in(splits[5], 71), 0)
    value_vectors = normal_values(splits[2], (HEAD_COUNT, FRAMES, GRID_ROWS, GRID_COLUMNS, HEAD_DIM), 1.0, 6.0, ((0, 4), (2, 8), (3, 8)))
    out_grad = normal_values(splits[3], (HEAD_COUNT, FRAMES, GRID_ROWS, GRID_COLUMNS, HEAD_DIM), 1.0, 6.0, ((0, 4), (2, 8), (3, 8)))
    cell_valid = draw_cell_valid(jax.random.fold_in(splits[5], 71), 0)
    return dict(queries=queries, key_vectors=key_vectors, value_vectors=value_vectors, out_grad=out_grad, cell_valid=cell_valid)


def window_mask(cell_rim, frames, tile_size):
    rim_span = 3 * tile_size
    offset = jnp.arange(rim_span)[None, :] - tile_size - jnp.arange(tile_size)[:, None]
    inside = jnp.abs(offset) <= tile_size
    key_ok = cell_rim == 1
    query_ok = key_ok[tile_size:2 * tile_size, tile_size:2 * tile_size]
    cell_pairs = inside[:, None, :, None] & inside[None, :, None, :] & key_ok[None, None] & query_ok[:, :, None, None]
    allowed = jnp.broadcast_to(cell_pairs[None, :, :, None], (frames, tile_size, tile_size, frames, rim_span, rim_span))
    allowed = allowed.reshape(frames * tile_size * tile_size, frames * rim_span * rim_span)
    query_live = jnp.broadcast_to(query_ok[None], (frames, tile_size, tile_size)).reshape(-1)
    return (allowed, query_live)

def tile_pass(query_tile, grad_tile, key_rim, value_rim, allowed, query_live):
    width = query_tile.shape[-1]
    score_scale = 1.0 / math.sqrt(width)
    query_rows = query_tile.reshape(-1, width)
    grad_rows = grad_tile.reshape(-1, width)
    key_rows = key_rim.reshape(-1, width)
    value_rows = value_rim.reshape(-1, width)
    scores = jnp.dot(query_rows, key_rows.T, preferred_element_type=jnp.float32) * score_scale
    masked = jnp.where(allowed, scores, -jnp.inf)
    row_max = jnp.where(query_live, lax.optimization_barrier(jnp.max(masked, axis=1)), 0.0)
    unnormed = jnp.where(allowed, jnp.exp(scores - row_max[:, None]), 0.0)
    row_total = lax.optimization_barrier(jnp.sum(unnormed, axis=1)) + jnp.where(query_live, 0.0, 1.0)
    probs = unnormed / row_total[:, None]
    probs_low = probs.astype(jnp.bfloat16)
    attended = jnp.dot(probs_low, value_rows, preferred_element_type=jnp.float32)
    row_delta = lax.optimization_barrier(jnp.sum(grad_rows.astype(jnp.float32) * attended, axis=1))
    dprobs = jnp.dot(grad_rows, value_rows.T, preferred_element_type=jnp.float32)
    dscores = probs * (dprobs - row_delta[:, None])
    dscores_low = dscores.astype(jnp.bfloat16)
    query_part = jnp.dot(dscores_low, key_rows, preferred_element_type=jnp.float32) * score_scale
    key_part = (jnp.dot(dscores_low.T, query_rows, preferred_element_type=jnp.float32) * score_scale).astype(jnp.bfloat16)
    value_part = jnp.dot(probs_low.T, grad_rows, preferred_element_type=jnp.float32).astype(jnp.bfloat16)
    return (query_part.reshape(query_tile.shape), key_part.reshape(key_rim.shape), value_part.reshape(value_rim.shape))

def reference(queries, key_vectors, value_vectors, out_grad, cell_valid):
    rim_span = 3 * TILE_CELLS
    tile_columns = GRID_COLUMNS // TILE_CELLS
    tile_total = GRID_ROWS // TILE_CELLS * tile_columns
    valid_padded = jnp.pad(cell_valid, TILE_CELLS)
    spatial_pad = ((0, 0), (TILE_CELLS, TILE_CELLS), (TILE_CELLS, TILE_CELLS), (0, 0))

    def per_head(inputs):
        query_head, key_head, value_head, grad_head = inputs
        key_padded = jnp.pad(key_head, spatial_pad)
        value_padded = jnp.pad(value_head, spatial_pad)

        def step(running, tile_index):
            query_acc, side_acc = running
            row_start = (tile_index // tile_columns * TILE_CELLS).astype(jnp.int32)
            col_start = (tile_index % tile_columns * TILE_CELLS).astype(jnp.int32)
            zero_index = jnp.zeros((), jnp.int32)
            query_tile = lax.dynamic_slice(query_head, (zero_index, row_start, col_start, zero_index), (FRAMES, TILE_CELLS, TILE_CELLS, HEAD_DIM))
            grad_tile = lax.dynamic_slice(grad_head, (zero_index, row_start, col_start, zero_index), (FRAMES, TILE_CELLS, TILE_CELLS, HEAD_DIM))
            key_rim = lax.dynamic_slice(key_padded, (zero_index, row_start, col_start, zero_index), (FRAMES, rim_span, rim_span, HEAD_DIM))
            value_rim = lax.dynamic_slice(value_padded, (zero_index, row_start, col_start, zero_index), (FRAMES, rim_span, rim_span, HEAD_DIM))
            cell_rim = lax.dynamic_slice(valid_padded, (row_start, col_start), (rim_span, rim_span))
            allowed, query_live = window_mask(cell_rim, FRAMES, TILE_CELLS)
            query_part, key_part, value_part = tile_pass(query_tile, grad_tile, key_rim, value_rim, allowed, query_live)
            query_acc = lax.dynamic_update_slice(query_acc, query_part, (zero_index, row_start, col_start, zero_index))
            where_side = (zero_index, zero_index, row_start, col_start, zero_index)
            current = lax.dynamic_slice(side_acc, where_side, (2, FRAMES, rim_span, rim_span, HEAD_DIM))
            added = current + jnp.stack([key_part, value_part]).astype(jnp.float32)
            side_acc = lax.dynamic_update_slice(side_acc, added, where_side)
            return ((query_acc, side_acc), None)
        start_state = (jnp.zeros((FRAMES, GRID_ROWS, GRID_COLUMNS, HEAD_DIM), jnp.float32), jnp.zeros((2, FRAMES, GRID_ROWS + 2 * TILE_CELLS, GRID_COLUMNS + 2 * TILE_CELLS, HEAD_DIM), jnp.float32))
        final_state, unused = lax.scan(step, start_state, jnp.arange(tile_total, dtype=jnp.int32))
        query_acc, side_acc = final_state
        side_sum = side_acc[:, :, TILE_CELLS:TILE_CELLS + GRID_ROWS, TILE_CELLS:TILE_CELLS + GRID_COLUMNS]
        return (query_acc.astype(jnp.bfloat16), side_sum[0].astype(jnp.bfloat16), side_sum[1].astype(jnp.bfloat16))
    query_grad, key_grad, value_grad = lax.map(per_head, (queries, key_vectors, value_vectors, out_grad))
    return (query_grad, key_grad, value_grad)
```

```python
import functools
import math

import jax
import jax.numpy as jnp
from jax import lax
from jax.experimental import pallas as pl
from jax.experimental.pallas import tpu as pltpu
from jax.sharding import PartitionSpec as P

MESH = pl.DeviceIdType.MESH
NEG = -1e30


def rows_by_rows(left, right):
    return lax.dot_general(
        left, right, (((1,), (1,)), ((), ())), preferred_element_type=jnp.float32
    )


def columns_by_columns(left, right):
    return lax.dot_general(
        left, right, (((0,), (0,)), ((), ())), preferred_element_type=jnp.float32
    )


def fold_rows(x, op):
    x = x.reshape(x.shape[0] // 8, 8, x.shape[1])
    return op(x, axis=0)


def kernel(
    sizes,
    q_hbm,
    k_hbm,
    v_hbm,
    g_hbm,
    valid_hbm,
    dq_hbm,
    dk_hbm,
    dv_hbm,
    kv,
    qg,
    part,
    from_rows,
    y_out,
    y_in,
    z_out,
    bias,
    s_buf,
    dp_buf,
    p_low,
    ds_low,
    scaled,
    by_lane,
    valid_ref,
    valid_sem,
    zin_send,
    zin_recv,
    yk_send,
    yk_recv,
    rk_send,
    rk_recv,
    rg_send,
    rg_recv,
    yg_send,
    yg_recv,
    zo_send,
    zo_recv,
):
    n_tp, n_sy, n_sx, heads, tile, frames, tokens, width = sizes
    n_y = n_sx // 2
    ring = 2 * n_tp
    hop = n_tp // 2
    half = heads // 2
    cells = tile * tile
    scale = 1.0 / math.sqrt(width)
    alpha = scale * math.log2(math.e)

    tp = lax.axis_index("tp")
    sy = lax.axis_index("sy")
    sx = lax.axis_index("sx")
    y = sx // 2
    zh = lax.rem(sx, 2)
    z = zh * n_tp + tp

    def z_peer(step):
        other = lax.rem(z + step + ring, ring)
        return other // n_tp, (lax.rem(other, n_tp), sy, y * 2 + other // n_tp)

    def y_peer(step):
        return (tp, sy, lax.rem(y + step + n_y, n_y) * 2 + zh)

    def row_peer(step):
        return (tp, lax.rem(sy + step + n_sy, n_sy), sx)

    up_side, up = z_peer(hop)
    down_side, down = z_peer(-hop)
    z_peers = (up, down)
    z_sides = (up_side, down_side)
    y_peers = (y_peer(-1), y_peer(1))
    row_peers = (row_peer(-1), row_peer(1))

    def copy(src, dst, send, recv, where):
        return pltpu.make_async_remote_copy(
            src_ref=src,
            dst_ref=dst,
            send_sem=send,
            recv_sem=recv,
            device_id=where,
            device_id_type=MESH,
        )

    barrier = pltpu.get_barrier_semaphore()
    for where in (*z_peers, *y_peers, *row_peers):
        pl.semaphore_signal(barrier, inc=1, device_id=where, device_id_type=MESH)
    fetch = pltpu.make_async_copy(valid_hbm, valid_ref, valid_sem)
    fetch.start()
    pl.semaphore_wait(barrier, 6)

    sources = (k_hbm, v_hbm, q_hbm, g_hbm)

    def zin_slot(t, h, side):
        if t < 2:
            return kv.at[t, h, 1, 1 + side]
        return qg.at[t - 2, h, side]

    def zin(t, h, way):
        which = zh if way == 0 else 1 - zh
        return copy(
            sources[t].at[which * half + h],
            zin_slot(t, h, zh),
            zin_send.at[t, h, way],
            zin_recv.at[t, h, zh],
            z_peers[way],
        )

    def zin_arrival(t, h, side):
        slot = zin_slot(t, h, side)
        return copy(slot, slot, zin_send.at[t, h, 0], zin_recv.at[t, h, side], up)

    def y_halo(t, h, way):
        src = kv.at[t, h, 1, 1 if way == 0 else 2]
        dst = kv.at[t, h, 1, 3 if way == 0 else 0]
        return copy(src, dst, yk_send.at[t, h, way], yk_recv.at[t, h, way], y_peers[way])

    def row_halo(t, h, way):
        return copy(
            kv.at[t, h, 1],
            kv.at[t, h, 2 if way == 0 else 0],
            rk_send.at[t, h, way],
            rk_recv.at[t, h, way],
            row_peers[way],
        )

    def row_grad(t, h, way):
        return copy(
            part.at[t, h, way],
            from_rows.at[t, h, way],
            rg_send.at[t, h, way],
            rg_recv.at[t, h, way],
            row_peers[way],
        )

    def y_grad(t, h, way):
        return copy(
            y_out.at[t, h, way],
            y_in.at[t, h, way],
            yg_send.at[t, h, way],
            yg_recv.at[t, h, way],
            y_peers[way],
        )

    in_first = jnp.logical_and(z >= hop, z < ring - hop)
    first_head = jnp.where(in_first, 0, half)
    results = (dk_hbm, dv_hbm, dq_hbm)

    def zout(t, h, way):
        return copy(
            z_out.at[t, h, z_sides[way]],
            results[t].at[first_head + h],
            zo_send.at[t, h, way],
            zo_recv.at[t, first_head + h],
            z_peers[way],
        )

    def start_in(tensors, h):
        for t in tensors:
            for way in (0, 1):
                zin(t, h, way).start()

    start_in((0, 1), 0)
    start_in((2, 3), 0)

    fetch.wait()
    valid = valid_ref[...].astype(jnp.float32).astype(jnp.bfloat16)
    grid_rows, grid_columns = valid.shape
    lane = lax.broadcasted_iota(jnp.int32, (cells, tokens), 1)
    cell = lax.broadcasted_iota(jnp.int32, (cells, tokens), 0)
    bits = tile.bit_length() - 1
    k_row, k_col = cell >> bits, cell & (tile - 1)
    q_row, q_col = (lane >> bits) & (tile - 1), lane & (tile - 1)
    sel_lane_r = lax.broadcasted_iota(jnp.int32, (cells, grid_rows), 1)
    sel_cell_r = lax.broadcasted_iota(jnp.int32, (cells, grid_rows), 0)
    sel_lane_c = lax.broadcasted_iota(jnp.int32, (cells, grid_columns), 1)
    sel_cell_c = lax.broadcasted_iota(jnp.int32, (cells, grid_columns), 0)
    ones = jnp.ones((grid_columns, tokens), jnp.bfloat16)

    def as_low(mask):
        return jnp.where(mask, 1.0, 0.0).astype(jnp.bfloat16)

    q_live = []
    for ct in range(2):
        col_lane = lax.broadcasted_iota(jnp.int32, (grid_columns, tokens), 1)
        col_cell = lax.broadcasted_iota(jnp.int32, (grid_columns, tokens), 0)
        pick = as_low(col_cell == (2 * y + ct) * tile + (col_lane & (tile - 1)))
        by_row = jnp.dot(valid, pick, preferred_element_type=jnp.float32)
        row_lane = lax.broadcasted_iota(jnp.int32, (grid_rows, tokens), 1)
        row_cell = lax.broadcasted_iota(jnp.int32, (grid_rows, tokens), 0)
        mine = row_cell == sy * tile + ((row_lane >> bits) & (tile - 1))
        q_live.append(jnp.sum(jnp.where(mine, by_row, 0.0), axis=0, keepdims=True))

    for r in range(3):
        pick_row = as_low(sel_lane_r == (sy - 1 + r) * tile + (sel_cell_r >> bits))
        by_cell = jnp.dot(pick_row, valid, preferred_element_type=jnp.float32)
        row_ok = jnp.abs((r - 1) * tile + k_row - q_row) <= tile
        for c in range(4):
            at_col = sel_lane_c == (2 * y - 1 + c) * tile + (sel_cell_c & (tile - 1))
            one = jnp.where(at_col, by_cell, 0.0).astype(jnp.bfloat16)
            k_live = jnp.dot(one, ones, preferred_element_type=jnp.float32)
            for ct in range(2):
                if 0 <= c - ct <= 2:
                    col_ok = jnp.abs((c - ct - 1) * tile + k_col - q_col) <= tile
                    ok = jnp.where(row_ok & col_ok, k_live * q_live[ct], 0.0)
                    bias[ct, r, c - ct] = jnp.where(ok > 0.5, 0.0, NEG)

    def relay_columns(h):
        for t in (0, 1):
            for way in (0, 1):
                zin_arrival(t, h, way).wait_recv()
                y_halo(t, h, way).start()

    def relay_rows(h):
        for t in (0, 1):
            for way in (0, 1):
                y_halo(t, h, way).wait_recv()
            for way in (0, 1):
                row_halo(t, h, way).start()

    def attend(h, ct):
        q = qg[0, h, ct]
        g = qg[1, h, ct]
        lanes = pl.ds(pl.multiple_of(ct * tokens, tokens), tokens)
        top = jnp.full((8, tokens), NEG, jnp.float32)
        for r in range(3):
            for c in range(3):
                s = rows_by_rows(kv[0, h, r, ct + c], q) * alpha
                s = s.reshape(frames, cells, tokens) + bias[ct, r, c][None]
                s = s.reshape(tokens, tokens)
                s_buf[r, c] = s
                top = jnp.maximum(top, fold_rows(s, jnp.max))
        top = jnp.max(top, axis=0, keepdims=True)

        total = jnp.zeros((8, tokens), jnp.float32)
        delta = jnp.zeros((8, tokens), jnp.float32)
        for r in range(3):
            for c in range(3):
                p = jnp.exp2(s_buf[r, c] - top)
                dp = rows_by_rows(kv[1, h, r, ct + c], g)
                s_buf[r, c] = p
                dp_buf[r, c] = dp
                p_low[r, ct + c, :, lanes] = p.astype(jnp.bfloat16)
                total = total + fold_rows(p, jnp.sum)
                delta = delta + fold_rows(p * dp, jnp.sum)
        total = jnp.sum(total, axis=0, keepdims=True)
        inverse = jnp.where(top > 0.1 * NEG, 1.0 / total, 0.0)
        delta = jnp.sum(delta, axis=0, keepdims=True) * inverse

        for r in range(3):
            for c in range(3):
                ds = s_buf[r, c] * (dp_buf[r, c] - delta)
                ds_low[r, ct + c, :, lanes] = ds.astype(jnp.bfloat16)

        inverse = jnp.broadcast_to(inverse, (width, tokens))
        by_token = inverse.T
        rows = lanes
        scaled[0, rows] = (q.astype(jnp.float32) * (by_token * scale)).astype(jnp.bfloat16)
        scaled[1, rows] = (g.astype(jnp.float32) * by_token).astype(jnp.bfloat16)
        by_lane[ct] = inverse * scale

    def key_products(h, r):
        where = {0: 0, 2: 1, 1: 2}[r]
        for t, low in ((0, ds_low), (1, p_low)):
            for c in range(4):
                first, last = max(c - 2, 0), min(c, 1)
                lanes = slice(first * tokens, (last + 1) * tokens)
                part[t, h, where, c] = jnp.dot(
                    low[r, c, :, lanes], scaled[t, lanes], preferred_element_type=jnp.float32
                ).astype(jnp.bfloat16)

    def query_products(h):
        for ct in range(2):
            lanes = slice(ct * tokens, (ct + 1) * tokens)
            dq = jnp.zeros((width, tokens), jnp.float32)
            for r in range(3):
                keys = kv[0, h, r, ct : ct + 3].reshape(3 * tokens, width)
                ds = ds_low[r, ct : ct + 3, :, lanes].reshape(3 * tokens, tokens)
                dq = dq + columns_by_columns(keys, ds)
            z_out[2, h, ct] = (dq * by_lane[ct]).T.astype(jnp.bfloat16)

    def add_rows(h):
        for t in (0, 1):
            for way in (0, 1):
                row_grad(t, h, way).wait_recv()
            for way, c in ((0, 0), (1, 3)):
                y_out[t, h, way] = (
                    part[t, h, 2, c].astype(jnp.float32)
                    + from_rows[t, h, 0, c].astype(jnp.float32)
                    + from_rows[t, h, 1, c].astype(jnp.float32)
                ).astype(jnp.bfloat16)
            for way in (0, 1):
                y_grad(t, h, way).start()

    def add_columns(h):
        for t in (0, 1):
            for way in (0, 1):
                y_grad(t, h, way).wait_recv()
            for side in (0, 1):
                z_out[t, h, side] = (
                    part[t, h, 2, 1 + side].astype(jnp.float32)
                    + from_rows[t, h, 0, 1 + side].astype(jnp.float32)
                    + from_rows[t, h, 1, 1 + side].astype(jnp.float32)
                    + y_in[t, h, 1 - side].astype(jnp.float32)
                ).astype(jnp.bfloat16)
            for way in (0, 1):
                zout(t, h, way).start()

    def wait_queries(h):
        for t in (2, 3):
            for way in (0, 1):
                zin_arrival(t, h, way).wait_recv()

    def wait_rows(h):
        for t in (0, 1):
            for way in (0, 1):
                row_halo(t, h, way).wait_recv()

    def attend_both(h):
        def step(ct, unused):
            attend(h, ct)
            return unused

        lax.fori_loop(0, 2, step, 0)

    def products(h):
        for way, r in ((0, 0), (1, 2)):
            key_products(h, r)
            for t in (0, 1):
                row_grad(t, h, way).start()
        key_products(h, 1)
        query_products(h)

    def send_queries(h):
        for way in (0, 1):
            zout(2, h, way).start()

    last = half - 1
    relay_columns(0)
    start_in((0, 1), 1)
    relay_rows(0)
    wait_queries(0)
    start_in((0, 1), 2)
    for h in range(half):
        wait_rows(h)
        if h >= 1:
            wait_queries(h)
        attend_both(h)
        if h == 0:
            relay_columns(1)
            start_in((2, 3), 1)
        if h == 1:
            add_columns(0)
        if h == 2:
            add_rows(1)
        products(h)
        if h == 0:
            relay_rows(1)
            relay_columns(2)
            start_in((2, 3), 2)
            send_queries(0)
            add_rows(0)
            relay_rows(2)
        else:
            send_queries(h)
    add_columns(last - 1)
    add_rows(last)
    for h in range(half):
        for way in (0, 1):
            for t in range(4):
                zin(t, h, way).wait_send()
            for t in range(2):
                y_halo(t, h, way).wait_send()
                row_halo(t, h, way).wait_send()
                row_grad(t, h, way).wait_send()
    add_columns(last)
    for h in range(half):
        for way in (0, 1):
            for t in range(2):
                y_grad(t, h, way).wait_send()
            for t in range(3):
                zout(t, h, way).wait_send()
    for t in range(3):
        for h in range(heads):
            slot = results[t].at[h]
            copy(slot, slot, zo_send.at[t, 0, 0], zo_recv.at[t, h], up).wait_recv()


def local(mesh_sizes, queries, key_vectors, value_vectors, out_grad, cell_valid):
    n_tp, n_sy, n_sx = mesh_sizes
    heads, frames, tile, _, width = queries.shape
    tokens = frames * tile * tile
    half = heads // 2
    cells = tile * tile
    sizes = (n_tp, n_sy, n_sx, heads, tile, frames, tokens, width)
    flat = [
        x.reshape(heads, tokens, width) for x in (queries, key_vectors, value_vectors, out_grad)
    ]
    low = jnp.bfloat16
    dma = pltpu.SemaphoreType.DMA
    out = pltpu.VMEM((heads, tokens, width), low)
    anywhere = pl.BlockSpec(memory_space=pl.ANY)
    results = pl.pallas_call(
        functools.partial(kernel, sizes),
        name="window_backward",
        out_shape=(out, out, out),
        in_specs=[pl.BlockSpec(memory_space=pltpu.HBM)] * 5,
        out_specs=(anywhere, anywhere, anywhere),
        scratch_shapes=[
            pltpu.VMEM((2, half, 3, 4, tokens, width), low),
            pltpu.VMEM((2, half, 2, tokens, width), low),
            pltpu.VMEM((2, half, 3, 4, tokens, width), low),
            pltpu.VMEM((2, half, 2, 4, tokens, width), low),
            pltpu.VMEM((2, half, 2, tokens, width), low),
            pltpu.VMEM((2, half, 2, tokens, width), low),
            pltpu.VMEM((3, half, 2, tokens, width), low),
            pltpu.VMEM((2, 3, 3, cells, tokens), jnp.float32),
            pltpu.VMEM((3, 3, tokens, tokens), jnp.float32),
            pltpu.VMEM((3, 3, tokens, tokens), jnp.float32),
            pltpu.VMEM((3, 4, tokens, 2 * tokens), low),
            pltpu.VMEM((3, 4, tokens, 2 * tokens), low),
            pltpu.VMEM((2, 2 * tokens, width), low),
            pltpu.VMEM((2, width, tokens), jnp.float32),
            pltpu.VMEM(cell_valid.shape, cell_valid.dtype),
            dma(()),
            dma((4, half, 2)),
            dma((4, half, 2)),
            dma((2, half, 2)),
            dma((2, half, 2)),
            dma((2, half, 2)),
            dma((2, half, 2)),
            dma((2, half, 2)),
            dma((2, half, 2)),
            dma((2, half, 2)),
            dma((2, half, 2)),
            dma((3, half, 2)),
            dma((3, heads)),
        ],
        compiler_params=pltpu.CompilerParams(
            collective_id=0, has_side_effects=True, vmem_limit_bytes=65_700_000
        ),
    )(*flat, cell_valid)
    return tuple(x.reshape(queries.shape) for x in results)


def solution(mesh):
    mesh_sizes = tuple(mesh.shape[name] for name in ("tp", "sy", "sx"))
    spec = P("tp", None, "sy", "sx", None)
    return jax.shard_map(
        functools.partial(local, mesh_sizes),
        mesh=mesh,
        in_specs=(spec, spec, spec, spec, P()),
        out_specs=(spec, spec, spec),
        check_vma=False,
    )
```
